32 devices in a mesh: ta: 8 (over y, x, core), gz: 4 (over z).
Axes of the slice: x: 2, y: 2, z: 4, core: 2. Of those that a mesh axis runs over, the one named last changes fastest.
Arguments:
- spinor: float32 [2, 4, 3, 16, 8, 768], P(None, None, None, 'ta', 'gz'), may hold values from -3 to 3
- links: float32 [4, 2, 3, 3, 16, 8, 768], P(None, None, None, None, 'ta', 'gz'), may hold values from -3.5 to 3.5
- clover: float32 [2, 2, 6, 6, 16, 8, 768], P(None, None, None, None, 'ta', 'gz'), may hold values from -1.2 to 1.2
Outputs:
- applied: float32 [2, 4, 3, 16, 8, 768], P(None, None, None, 'ta', 'gz')
- force: float32 [4, 2, 3, 3, 16, 8, 768], P(None, None, None, None, 'ta', 'gz')
The draws below stay inside these ranges and needn't reach their ends.
All inputs are finite; a program needn't handle non-finite values.
Results may differ from the reference program's by a relative error of at most 0.0001.
Values sent between devices are 32-bit elements; how exact they have to be, the bound alone decides.
A program may use at most 64 MiB of HBM per device.

```python
import jax
import jax.numpy as jnp

NY = 12
NX = 64
PLANE = 768
NT = 16
NZ = 8


def shard_levels(stream_key, extent, pieces, least, largest):
    def one(dim, shards_of):
        heights = jax.random.uniform(jax.random.fold_in(jax.random.fold_in(stream_key, 6), dim), (shards_of,), jnp.float32, least / len(pieces), largest / len(pieces))
        return jnp.repeat(jnp.exp(heights), extent[dim] // shards_of).reshape((-1,) + (1,) * (len(extent) - dim - 1))

    gain = one(*pieces[0])
    for cut in pieces[1:]:
        gain = gain * one(*cut)
    return gain


def centred(key, extent, spread, limit, shards=(), kind=jnp.bfloat16):
    array = jax.random.normal(key, extent, jnp.float32) * spread
    if len(shards) > 0:
        array = shard_levels(key, extent, shards, -0.22, 0.18) * array
    return jnp.clip(array, min=-limit, max=limit).astype(kind)


def setup_inputs(seed: int = 0) -> dict:
    key_of = jax.random.split(jax.random.key(seed), 4)
    spinor = centred(key_of[0], (2, 4, 3, NT, NZ, PLANE), 0.5, 3.0, ((3, 8), (4, 4)), jnp.float32)
    links = centred(key_of[1], (4, 2, 3, 3, NT, NZ, PLANE), 3 ** -0.5, 3.5, ((4, 8), (5, 4)), jnp.float32)
    clover = centred(key_of[2], (2, 2, 6, 6, NT, NZ, PLANE), 0.2, 1.2, ((4, 8), (5, 4)), jnp.float32)
    return {"spinor": spinor, "links": links, "clover": clover}


bare_mass = -0.25

gamma_table = (
    ((3, 0.0, -1.0), (2, 0.0, -1.0), (1, 0.0, 1.0), (0, 0.0, 1.0)),
    ((3, -1.0, 0.0), (2, 1.0, 0.0), (1, 1.0, 0.0), (0, -1.0, 0.0)),
    ((2, 0.0, -1.0), (3, 0.0, 1.0), (0, 0.0, 1.0), (1, 0.0, -1.0)),
    ((2, 1.0, 0.0), (3, 1.0, 0.0), (0, 1.0, 0.0), (1, 1.0, 0.0)),
)


def apply_gamma(hop_dir, field):
    parts_re = []
    parts_im = []
    for spin_row in range(4):
        source, phase_re, phase_im = gamma_table[hop_dir][spin_row]
        source_re = field[0, source]
        source_im = field[1, source]
        if phase_im == 0.0:
            parts_re.append(phase_re * source_re)
            parts_im.append(phase_re * source_im)
        else:
            parts_re.append(-phase_im * source_im)
            parts_im.append(phase_im * source_re)
    return jnp.stack([jnp.stack(parts_re), jnp.stack(parts_im)])


def project(hop_dir, field, sign):
    return field + sign * apply_gamma(hop_dir, field)


def color_apply(link, field, dagger):
    link_re = link[0]
    link_im = link[1]
    if dagger:
        link_re = jnp.swapaxes(link_re, 0, 1)
        link_im = -jnp.swapaxes(link_im, 0, 1)
    matrix_re = link_re[None]
    matrix_im = link_im[None]
    field_re = field[0][:, None]
    field_im = field[1][:, None]
    out_re = jnp.sum(matrix_re * field_re - matrix_im * field_im, axis=2)
    out_im = jnp.sum(matrix_re * field_im + matrix_im * field_re, axis=2)
    return jnp.stack([out_re, out_im])


def clover_apply(clover, field):
    halves = field.reshape((2, 2, 6) + field.shape[3:])
    field_re = halves[0][:, None]
    field_im = halves[1][:, None]
    out_re = jnp.sum(clover[0] * field_re - clover[1] * field_im, axis=2)
    out_im = jnp.sum(clover[0] * field_im + clover[1] * field_re, axis=2)
    return jnp.stack([out_re, out_im]).reshape(field.shape)


def spin_outer(left, right):
    left_re = left[0][:, :, None]
    left_im = left[1][:, :, None]
    right_re = right[0][:, None]
    right_im = right[1][:, None]
    out_re = jnp.sum(left_re * right_re + left_im * right_im, axis=0)
    out_im = jnp.sum(left_im * right_re - left_re * right_im, axis=0)
    return jnp.stack([out_re, out_im])


def color_product(first, second):
    first_re = first[0][:, :, None]
    first_im = first[1][:, :, None]
    second_re = second[0][None]
    second_im = second[1][None]
    out_re = jnp.sum(first_re * second_re - first_im * second_im, axis=1)
    out_im = jnp.sum(first_re * second_im + first_im * second_re, axis=1)
    return jnp.stack([out_re, out_im])


def traceless(matrix):
    mat_re = matrix[0]
    mat_im = matrix[1]
    anti_re = 0.5 * (mat_re - jnp.swapaxes(mat_re, 0, 1))
    anti_im = 0.5 * (mat_im + jnp.swapaxes(mat_im, 0, 1))
    trace_third = (mat_im[0, 0] + mat_im[1, 1] + mat_im[2, 2]) / 3.0
    identity = jnp.eye(3, dtype=jnp.float32).reshape((3, 3) + (1,) * (mat_re.ndim - 2))
    return jnp.stack([anti_re, anti_im - identity * trace_third])


def along_plane(field, hop_dir, step):
    shape = field.shape
    grid = field.reshape(shape[:-1] + (NY, NX))
    if hop_dir == 0:
        grid = jnp.roll(grid, -step, axis=-1)
    else:
        grid = jnp.roll(grid, -step, axis=-2)
    return grid.reshape(shape)


def neighbor(field, hop_dir, step, fermion):
    if hop_dir < 2:
        return along_plane(field, hop_dir, step)
    if hop_dir == 2:
        return jnp.roll(field, -step, axis=4)
    moved = jnp.roll(field, -step, axis=3)
    if fermion:
        boundary = field.shape[3] - 1 if step == 1 else 0
        moved = moved.at[:, :, :, boundary].multiply(-1.0)
    return moved


def reference(spinor, links, clover):
    hopping = jnp.zeros_like(spinor)
    forward_half = []
    for hop_dir in range(4):
        ahead_proj = project(hop_dir, neighbor(spinor, hop_dir, 1, True), -1.0)
        forward_half.append(ahead_proj)
        behind = neighbor(spinor, hop_dir, -1, True)
        back_link = neighbor(links[hop_dir], hop_dir, -1, False)
        hopping = hopping + color_apply(links[hop_dir], ahead_proj, False) + color_apply(back_link, project(hop_dir, behind, 1.0), True)
    applied = (4.0 + bare_mass) * spinor + clover_apply(clover, spinor) - 0.5 * hopping
    forces = []
    for hop_dir in range(4):
        ahead_applied = neighbor(applied, hop_dir, 1, True)
        summed = spin_outer(forward_half[hop_dir], applied) + spin_outer(project(hop_dir, ahead_applied, 1.0), spinor)
        forces.append(traceless(color_product(links[hop_dir], summed)))
    return applied, jnp.stack(forces)
```

```python
import jax
import jax.numpy as jnp
from jax import lax
from jax.experimental import pallas as pl
from jax.experimental.pallas import tpu as pltpu
from jax.sharding import PartitionSpec as P

NX = 64
LANES = 128
TILE = 8
MESH = pl.DeviceIdType.MESH

bare_mass = -0.25
gamma_table = (
    ((3, 0.0, -1.0), (2, 0.0, -1.0), (1, 0.0, 1.0), (0, 0.0, 1.0)),
    ((3, -1.0, 0.0), (2, 1.0, 0.0), (1, 1.0, 0.0), (0, -1.0, 0.0)),
    ((2, 0.0, -1.0), (3, 0.0, 1.0), (0, 0.0, 1.0), (1, 0.0, -1.0)),
    ((2, 1.0, 0.0), (3, 1.0, 0.0), (0, 1.0, 0.0), (1, 1.0, 0.0)),
)


def add_signed(a, b, positive):
    return a + b if positive else a - b


def add_phase(a, b, phase_re, phase_im):
    if phase_im == 0.0:
        up = phase_re > 0
        return (add_signed(a[0], b[0], up), add_signed(a[1], b[1], up))
    up = phase_im > 0
    return (add_signed(a[0], b[1], not up), add_signed(a[1], b[0], up))


def half(mu, field, sign):
    out = []
    for s in range(2):
        source, p_re, p_im = gamma_table[mu][s]
        out.append(
            [add_phase(field[s][c], field[source][c], sign * p_re, sign * p_im) for c in range(3)]
        )
    return out


def add_whole(mu, total, halves, sign):
    out = [[add_phase(total[s][c], halves[s][c], 1.0, 0.0) for c in range(3)] for s in range(2)]
    for s in (2, 3):
        source, p_re, p_im = gamma_table[mu][s]
        out.append(
            [add_phase(total[s][c], halves[source][c], sign * p_re, sign * p_im) for c in range(3)]
        )
    return out


def csum(terms):
    total = terms[0]
    for term in terms[1:]:
        total = total + term
    return total


def mat_vec(link, vec, dagger):
    out = []
    for s in range(2):
        rows = []
        for a in range(3):
            re, im = [], []
            for b in range(3):
                h = vec[s][b]
                if dagger:
                    m = link[b][a]
                    re.append(m[0] * h[0] + m[1] * h[1])
                    im.append(m[0] * h[1] - m[1] * h[0])
                else:
                    m = link[a][b]
                    re.append(m[0] * h[0] - m[1] * h[1])
                    im.append(m[0] * h[1] + m[1] * h[0])
            rows.append((csum(re), csum(im)))
        out.append(rows)
    return out


def kernel(nt, nz, x_hbm, u_hbm, c_hbm, out_ref, force_ref, psi, link, clov, hm, hp, bl, sh_hm,
           sh_bl, prod, acc, hphi, sh_hphi, face_out, face_in, in_sem, send_sem, recv_sem):
    rows = psi.shape[1]
    face_t = rows // nt
    face_z = rows // nz
    chunks = rows // TILE
    t_place, z_place = lax.axis_index("ta"), lax.axis_index("gz")
    t_count, z_count = lax.axis_size("ta"), lax.axis_size("gz")
    t_next = (lax.rem(t_place + 1, t_count), z_place)
    t_prev = (lax.rem(t_place + t_count - 1, t_count), z_place)
    z_next = (t_place, lax.rem(z_place + 1, z_count))
    z_prev = (t_place, lax.rem(z_place + z_count - 1, z_count))
    low_sign = jnp.where(t_place == 0, -1.0, 1.0).astype(jnp.float32)
    high_sign = jnp.where(t_place == t_count - 1, -1.0, 1.0).astype(jnp.float32)

    barrier = pltpu.get_barrier_semaphore()
    for target in (t_next, t_prev, z_next, z_prev):
        pl.semaphore_signal(barrier, inc=1, device_id=target, device_id_type=MESH)

    loads = [pltpu.make_async_copy(x_hbm, psi, in_sem.at[0])]
    for mu in range(4):
        part = pl.ds(18 * mu, 18)
        loads.append(pltpu.make_async_copy(u_hbm.at[part], link.at[part], in_sem.at[1 + mu]))
    loads.append(pltpu.make_async_copy(c_hbm, clov, in_sem.at[5]))
    for n in (0, 4, 3, 1, 2, 5):
        loads[n].start()

    def window(v):
        return pl.ds(pl.multiple_of(v * TILE, TILE), TILE)

    def load_spinor(ref, at):
        return [[(ref[3 * s + c, at, :], ref[12 + 3 * s + c, at, :]) for c in range(3)] for s in range(4)]

    def load_half(ref, mu, at):
        return [[(ref[mu, 3 * s + c, at, :], ref[mu, 6 + 3 * s + c, at, :]) for c in range(3)] for s in range(2)]

    def store_half(ref, mu, at, value):
        for s in range(2):
            for c in range(3):
                ref[mu, 3 * s + c, at, :] = value[s][c][0]
                ref[mu, 6 + 3 * s + c, at, :] = value[s][c][1]

    def load_link(mu, at):
        return [[(link[18 * mu + 3 * a + b, at, :], link[18 * mu + 9 + 3 * a + b, at, :]) for b in range(3)] for a in range(3)]

    lane = lax.broadcasted_iota(jnp.int32, (rows, LANES), 1)
    row = lax.broadcasted_iota(jnp.int32, (rows, LANES), 0)
    lane_in = lax.rem(lane, NX)
    row_in = lax.rem(row, face_t)
    upper = lane >= NX

    def shift_x1(value, step):
        if step == 1:
            near, far = pltpu.roll(value, LANES - 1, 1), pltpu.roll(value, NX - 1, 1)
            return jnp.where(lane_in == NX - 1, far, near)
        near, far = pltpu.roll(value, 1, 1), pltpu.roll(value, LANES - NX + 1, 1)
        return jnp.where(lane_in == 0, far, near)

    def shift_x2(value, step):
        turned = pltpu.roll(value, NX, 1)
        if step == 1:
            near = pltpu.roll(turned, rows - nz, 0)
            far = pltpu.roll(turned, face_t - nz, 0)
            moved = jnp.where(row_in >= face_t - nz, far, near)
            return jnp.where(upper, moved, turned)
        near = pltpu.roll(turned, nz, 0)
        far = pltpu.roll(turned, rows - face_t + nz, 0)
        moved = jnp.where(row_in < nz, far, near)
        return jnp.where(upper, turned, moved)

    def z_ahead(src, dst, c):
        for z in range(nz - 1):
            dst[2, c, pl.ds(z, face_z, nz), :] = src[2, c, pl.ds(z + 1, face_z, nz), :]

    def z_behind(src, dst, c):
        for z in range(1, nz):
            dst[2, c, pl.ds(z, face_z, nz), :] = src[2, c, pl.ds(z - 1, face_z, nz), :]

    def t_ahead(src, dst, c):
        dst[3, c, pl.ds(0, rows - face_t), :] = src[3, c, pl.ds(face_t, rows - face_t), :]

    def t_behind(src, dst, c):
        dst[3, c, pl.ds(face_t, rows - face_t), :] = src[3, c, pl.ds(0, rows - face_t), :]

    def for_each(count, body):
        def step(i, carry):
            body(i)
            return carry

        lax.fori_loop(0, count, step, 0)

    targets = (t_prev, t_next, z_prev, z_next, t_prev, z_prev)
    sends = [
        pltpu.make_async_remote_copy(
            src_ref=face_out.at[k], dst_ref=face_in.at[k], send_sem=send_sem.at[k],
            recv_sem=recv_sem.at[k], device_id=targets[k], device_id_type=MESH,
        )
        for k in range(6)
    ]

    def project(mu, v):
        at = window(v)
        field = load_spinor(psi, at)
        store_half(hm, mu, at, half(mu, field, -1.0))
        ahead = half(mu, field, 1.0)
        store_half(hp, mu, at, ahead)
        store_half(bl, mu, at, mat_vec(load_link(mu, at), ahead, True))

    loads[0].wait()
    loads[4].wait()
    for_each(chunks, lambda v: project(3, v))

    for c in range(12):
        face_out[0, c, 0:face_t, :] = hm[3, c, 0:face_t, :]
        face_out[1, c, 0:face_t, :] = bl[3, c, rows - face_t:rows, :]
    pl.semaphore_wait(barrier, 4)
    sends[0].start()
    sends[1].start()
    loads[3].wait()
    for_each(chunks, lambda v: project(2, v))
    for c in range(12):
        face_out[2, c, 0:face_z, :] = hm[2, c, pl.ds(0, face_z, nz), :]
        face_out[3, c, 0:face_z, :] = bl[2, c, pl.ds(nz - 1, face_z, nz), :]
    sends[2].start()
    sends[3].start()

    loads[1].wait()
    for_each(chunks, lambda v: project(0, v))
    loads[2].wait()
    for_each(chunks, lambda v: project(1, v))

    def shifts(c):
        sh_hm[0, c] = shift_x1(hm[0, c], 1)
        sh_bl[0, c] = shift_x1(bl[0, c], -1)
        sh_hm[1, c] = shift_x2(hm[1, c], 1)
        sh_bl[1, c] = shift_x2(bl[1, c], -1)
        z_ahead(hm, sh_hm, c)
        z_behind(bl, sh_bl, c)
        t_ahead(hm, sh_hm, c)
        t_behind(bl, sh_bl, c)

    for_each(12, shifts)

    def hop(mu, at, total):
        ahead = mat_vec(load_link(mu, at), load_half(sh_hm, mu, at), False)
        store_half(prod, mu, at, ahead)
        total = add_whole(mu, total, ahead, -1.0)
        return add_whole(mu, total, load_half(sh_bl, mu, at), 1.0)

    zero = jnp.zeros((TILE, LANES), jnp.float32)

    loads[5].wait()

    def local(v):
        at = window(v)
        field = load_spinor(psi, at)
        total = [[(zero, zero)] * 3 for _ in range(4)]
        for mu in (0, 1):
            total = hop(mu, at, total)
        for s in range(4):
            for c in range(3):
                base = 36 * (s // 2) + 6 * (3 * (s % 2) + c)
                re = (4.0 + bare_mass) * field[s][c][0] - 0.5 * total[s][c][0]
                im = (4.0 + bare_mass) * field[s][c][1] - 0.5 * total[s][c][1]
                for k in range(6):
                    other = field[2 * (s // 2) + k // 3][k % 3]
                    c_re = clov[base + k, at, :]
                    c_im = clov[72 + base + k, at, :]
                    re = re + (c_re * other[0] - c_im * other[1])
                    im = im + (c_re * other[1] + c_im * other[0])
                acc[3 * s + c, at, :] = re
                acc[12 + 3 * s + c, at, :] = im

    for_each(chunks, local)

    for k in range(4):
        sends[k].wait_recv()

    for c in range(12):
        sh_hm[3, c, pl.ds(rows - face_t, face_t), :] = face_in[0, c, 0:face_t, :] * high_sign
        sh_bl[3, c, pl.ds(0, face_t), :] = face_in[1, c, 0:face_t, :] * low_sign
        sh_hm[2, c, pl.ds(nz - 1, face_z, nz), :] = face_in[2, c, 0:face_z, :]
        sh_bl[2, c, pl.ds(0, face_z, nz), :] = face_in[3, c, 0:face_z, :]

    def finish(v):
        at = window(v)
        total = [[(zero, zero)] * 3 for _ in range(4)]
        for mu in (2, 3):
            total = hop(mu, at, total)
        held = load_spinor(acc, at)
        phi = [
            [(held[s][c][0] - 0.5 * total[s][c][0], held[s][c][1] - 0.5 * total[s][c][1]) for c in range(3)]
            for s in range(4)
        ]
        for s in range(4):
            for c in range(3):
                out_ref[3 * s + c, at, :] = phi[s][c][0]
                out_ref[12 + 3 * s + c, at, :] = phi[s][c][1]
        for mu in range(4):
            store_half(hphi, mu, at, half(mu, phi, 1.0))

    for_each(chunks, finish)

    for c in range(12):
        face_out[4, c, 0:face_t, :] = hphi[3, c, 0:face_t, :]
        face_out[5, c, 0:face_z, :] = hphi[2, c, pl.ds(0, face_z, nz), :]
    sends[4].start()
    sends[5].start()

    def shifts_phi(c):
        sh_hphi[0, c] = shift_x1(hphi[0, c], 1)
        sh_hphi[1, c] = shift_x2(hphi[1, c], 1)
        z_ahead(hphi, sh_hphi, c)
        t_ahead(hphi, sh_hphi, c)

    for_each(12, shifts_phi)

    def force(mu, v):
        at = window(v)
        second = mat_vec(load_link(mu, at), load_half(sh_hphi, mu, at), False)
        second_right = load_half(hp, mu, at)
        first = load_half(prod, mu, at)
        first_right = half(mu, load_spinor(out_ref, at), -1.0)
        pairs = [(first[s], first_right[s]) for s in range(2)] + [(second[s], second_right[s]) for s in range(2)]

        def w_re(a, b):
            return csum([l[a][0] * r[b][0] + l[a][1] * r[b][1] for l, r in pairs])

        def w_im(a, b):
            return csum([l[a][1] * r[b][0] - l[a][0] * r[b][1] for l, r in pairs])

        diag = [w_im(a, a) for a in range(3)]
        third = (diag[0] + diag[1] + diag[2]) * (1.0 / 3.0)
        base = 18 * mu
        for a in range(3):
            force_ref[base + 4 * a, at, :] = zero
            force_ref[base + 9 + 4 * a, at, :] = diag[a] - third
            for b in range(a + 1, 3):
                re = 0.5 * (w_re(a, b) - w_re(b, a))
                im = 0.5 * (w_im(a, b) + w_im(b, a))
                force_ref[base + 3 * a + b, at, :] = re
                force_ref[base + 3 * b + a, at, :] = -re
                force_ref[base + 9 + 3 * a + b, at, :] = im
                force_ref[base + 9 + 3 * b + a, at, :] = im

    for_each(chunks, lambda v: force(0, v))
    for_each(chunks, lambda v: force(1, v))

    for k in (4, 5):
        sends[k].wait_recv()
    for c in range(12):
        sh_hphi[3, c, pl.ds(rows - face_t, face_t), :] = face_in[4, c, 0:face_t, :] * high_sign
        sh_hphi[2, c, pl.ds(nz - 1, face_z, nz), :] = face_in[5, c, 0:face_z, :]
    for_each(chunks, lambda v: force(2, v))
    for_each(chunks, lambda v: force(3, v))
    for k in range(6):
        sends[k].wait_send()


def to_rows(array):
    nt, nz, plane = array.shape[-3:]
    parts = plane // LANES
    grid = array.reshape((-1, nt, nz, parts, LANES))
    return jnp.swapaxes(grid, 2, 3).reshape((-1, nt * parts * nz, LANES))


def from_rows(rows, shape):
    nt, nz, plane = shape[-3:]
    grid = rows.reshape((-1, nt, plane // LANES, nz, LANES))
    return jnp.swapaxes(grid, 2, 3).reshape(shape)


def body(spinor, links, clover):
    nt, nz = spinor.shape[3], spinor.shape[4]
    x, u, c = to_rows(spinor), to_rows(links), to_rows(clover)
    rows = x.shape[1]
    face = max(rows // nt, rows // nz)

    def halves():
        return pltpu.VMEM((4, 12, rows, LANES), jnp.float32)

    applied, force = pl.pallas_call(
        lambda *refs: kernel(nt, nz, *refs),
        name="wilson",
        out_shape=(
            jax.ShapeDtypeStruct(x.shape, jnp.float32),
            jax.ShapeDtypeStruct(u.shape, jnp.float32),
        ),
        in_specs=[pl.BlockSpec(memory_space=pl.ANY)] * 3,
        out_specs=(pl.BlockSpec(memory_space=pltpu.VMEM),) * 2,
        scratch_shapes=[
            pltpu.VMEM(x.shape, jnp.float32),
            pltpu.VMEM(u.shape, jnp.float32),
            pltpu.VMEM(c.shape, jnp.float32),
            halves(), halves(), halves(), halves(), halves(), halves(),
            pltpu.VMEM(x.shape, jnp.float32),
            halves(), halves(),
            pltpu.VMEM((6, 12, face, LANES), jnp.float32),
            pltpu.VMEM((6, 12, face, LANES), jnp.float32),
            pltpu.SemaphoreType.DMA((6,)),
            pltpu.SemaphoreType.DMA((6,)),
            pltpu.SemaphoreType.DMA((6,)),
        ],
        compiler_params=pltpu.CompilerParams(collective_id=0, has_side_effects=True),
    )(x, u, c)
    return from_rows(applied, spinor.shape), from_rows(force, links.shape)


def solution(mesh):
    return jax.shard_map(
        body,
        mesh=mesh,
        in_specs=(
            P(None, None, None, "ta", "gz", None),
            P(None, None, None, None, "ta", "gz", None),
            P(None, None, None, None, "ta", "gz", None),
        ),
        out_specs=(
            P(None, None, None, "ta", "gz", None),
            P(None, None, None, None, "ta", "gz", None),
        ),
        check_vma=False,
    )
```

```python
import jax
import jax.numpy as jnp
from jax import lax
from jax.experimental import pallas as pl
from jax.experimental.pallas import tpu as pltpu
from jax.sharding import PartitionSpec as P

NX = 64
LANES = 128
TILE = 8
MESH = pl.DeviceIdType.MESH

bare_mass = -0.25
gamma_table = (
    ((3, 0.0, -1.0), (2, 0.0, -1.0), (1, 0.0, 1.0), (0, 0.0, 1.0)),
    ((3, -1.0, 0.0), (2, 1.0, 0.0), (1, 1.0, 0.0), (0, -1.0, 0.0)),
    ((2, 0.0, -1.0), (3, 0.0, 1.0), (0, 0.0, 1.0), (1, 0.0, -1.0)),
    ((2, 1.0, 0.0), (3, 1.0, 0.0), (0, 1.0, 0.0), (1, 1.0, 0.0)),
)


def add_signed(a, b, positive):
    return a + b if positive else a - b


def add_phase(a, b, phase_re, phase_im):
    if phase_im == 0.0:
        up = phase_re > 0
        return (add_signed(a[0], b[0], up), add_signed(a[1], b[1], up))
    up = phase_im > 0
    return (add_signed(a[0], b[1], not up), add_signed(a[1], b[0], up))


def half(mu, field, sign):
    out = []
    for s in range(2):
        source, p_re, p_im = gamma_table[mu][s]
        out.append(
            [add_phase(field[s][c], field[source][c], sign * p_re, sign * p_im) for c in range(3)]
        )
    return out


def add_whole(mu, total, halves, sign):
    out = [[add_phase(total[s][c], halves[s][c], 1.0, 0.0) for c in range(3)] for s in range(2)]
    for s in (2, 3):
        source, p_re, p_im = gamma_table[mu][s]
        out.append(
            [add_phase(total[s][c], halves[source][c], sign * p_re, sign * p_im) for c in range(3)]
        )
    return out


def csum(terms):
    total = terms[0]
    for term in terms[1:]:
        total = total + term
    return total


def mat_vec(link, vec, dagger):
    out = []
    for s in range(2):
        rows = []
        for a in range(3):
            re, im = [], []
            for b in range(3):
                h = vec[s][b]
                if dagger:
                    m = link[b][a]
                    re.append(m[0] * h[0] + m[1] * h[1])
                    im.append(m[0] * h[1] - m[1] * h[0])
                else:
                    m = link[a][b]
                    re.append(m[0] * h[0] - m[1] * h[1])
                    im.append(m[0] * h[1] + m[1] * h[0])
            rows.append((csum(re), csum(im)))
        out.append(rows)
    return out


def flat(ref):
    return ref.reshape(ref.shape[0], ref.shape[1] * ref.shape[2], ref.shape[3])


def parts_of(whole, held):
    parts = whole.shape[-1] // LANES
    for t in range(whole.shape[-3]):
        for q in range(parts):
            yield whole.at[:, t, :, pl.ds(LANES * q, LANES)], held.at[:, parts * t + q]


def kernel(nt, nz, x_hbm, u_hbm, c_hbm, out_hbm, force_hbm, psi_in, link_in, clov_in, phi_out, force_out, hm, hp, bl,
           sh_hm, sh_bl, prod, acc, hphi, sh_hphi, face_out, face_in, in_sem, out_sem, send_sem, recv_sem):
    psi, link, clov, out_ref, force_ref = map(flat, (psi_in, link_in, clov_in, phi_out, force_out))
    rows = psi.shape[1]
    face_t = rows // nt
    face_z = rows // nz
    chunks = rows // TILE
    t_place, z_place = lax.axis_index("ta"), lax.axis_index("gz")
    t_count, z_count = lax.axis_size("ta"), lax.axis_size("gz")
    t_next = (lax.rem(t_place + 1, t_count), z_place)
    t_prev = (lax.rem(t_place + t_count - 1, t_count), z_place)
    z_next = (t_place, lax.rem(z_place + 1, z_count))
    z_prev = (t_place, lax.rem(z_place + z_count - 1, z_count))
    low_sign = jnp.where(t_place == 0, -1.0, 1.0).astype(jnp.float32)
    high_sign = jnp.where(t_place == t_count - 1, -1.0, 1.0).astype(jnp.float32)

    barrier = pltpu.get_barrier_semaphore()
    for target in (t_next, t_prev, z_next, z_prev):
        pl.semaphore_signal(barrier, inc=1, device_id=target, device_id_type=MESH)

    groups = [(x_hbm, psi_in)]
    for mu in range(4):
        part = pl.ds(18 * mu, 18)
        groups.append((u_hbm.at[part], link_in.at[part]))
    groups.append((c_hbm, clov_in))
    for n in (0, 4, 3, 1, 2, 5):
        for src, dst in parts_of(*groups[n]):
            pltpu.make_async_copy(src, dst, in_sem.at[n]).start()

    def arrived(n):
        held = groups[n][1]
        pltpu.make_async_copy(held, held, in_sem.at[n]).wait()

    results = [(out_hbm, phi_out)]
    for mu in range(4):
        part = pl.ds(18 * mu, 18)
        results.append((force_hbm.at[part], force_out.at[part]))

    def leave(n):
        for dst, src in parts_of(*results[n]):
            pltpu.make_async_copy(src, dst, out_sem.at[n]).start()

    def left(n):
        held = results[n][1]
        pltpu.make_async_copy(held, held, out_sem.at[n]).wait()

    def window(v):
        return pl.ds(pl.multiple_of(v * TILE, TILE), TILE)

    def load_spinor(ref, at):
        return [[(ref[3 * s + c, at, :], ref[12 + 3 * s + c, at, :]) for c in range(3)] for s in range(4)]

    def load_half(ref, mu, at):
        return [[(ref[mu, 3 * s + c, at, :], ref[mu, 6 + 3 * s + c, at, :]) for c in range(3)] for s in range(2)]

    def store_half(ref, mu, at, value):
        for s in range(2):
            for c in range(3):
                ref[mu, 3 * s + c, at, :] = value[s][c][0]
                ref[mu, 6 + 3 * s + c, at, :] = value[s][c][1]

    def load_link(mu, at):
        return [[(link[18 * mu + 3 * a + b, at, :], link[18 * mu + 9 + 3 * a + b, at, :]) for b in range(3)] for a in range(3)]

    lane = lax.broadcasted_iota(jnp.int32, (rows, LANES), 1)
    row = lax.broadcasted_iota(jnp.int32, (rows, LANES), 0)
    lane_in = lax.rem(lane, NX)
    row_in = lax.rem(row, face_t)
    upper = lane >= NX

    def shift_x1(value, step):
        if step == 1:
            near, far = pltpu.roll(value, LANES - 1, 1), pltpu.roll(value, NX - 1, 1)
            return jnp.where(lane_in == NX - 1, far, near)
        near, far = pltpu.roll(value, 1, 1), pltpu.roll(value, LANES - NX + 1, 1)
        return jnp.where(lane_in == 0, far, near)

    def shift_x2(value, step):
        turned = pltpu.roll(value, NX, 1)
        if step == 1:
            near = pltpu.roll(turned, rows - nz, 0)
            far = pltpu.roll(turned, face_t - nz, 0)
            moved = jnp.where(row_in >= face_t - nz, far, near)
            return jnp.where(upper, moved, turned)
        near = pltpu.roll(turned, nz, 0)
        far = pltpu.roll(turned, rows - face_t + nz, 0)
        moved = jnp.where(row_in < nz, far, near)
        return jnp.where(upper, turned, moved)

    def z_ahead(src, dst, c):
        for z in range(nz - 1):
            dst[2, c, pl.ds(z, face_z, nz), :] = src[2, c, pl.ds(z + 1, face_z, nz), :]

    def z_behind(src, dst, c):
        for z in range(1, nz):
            dst[2, c, pl.ds(z, face_z, nz), :] = src[2, c, pl.ds(z - 1, face_z, nz), :]

    def t_ahead(src, dst, c):
        dst[3, c, pl.ds(0, rows - face_t), :] = src[3, c, pl.ds(face_t, rows - face_t), :]

    def t_behind(src, dst, c):
        dst[3, c, pl.ds(face_t, rows - face_t), :] = src[3, c, pl.ds(0, rows - face_t), :]

    def for_each(count, body):
        def step(i, carry):
            body(i)
            return carry

        lax.fori_loop(0, count, step, 0)

    targets = (t_prev, t_next, z_prev, z_next, t_prev, z_prev)
    sends = [
        pltpu.make_async_remote_copy(
            src_ref=face_out.at[k], dst_ref=face_in.at[k], send_sem=send_sem.at[k],
            recv_sem=recv_sem.at[k], device_id=targets[k], device_id_type=MESH,
        )
        for k in range(6)
    ]

    def project(mu, v):
        at = window(v)
        field = load_spinor(psi, at)
        store_half(hm, mu, at, half(mu, field, -1.0))
        ahead = half(mu, field, 1.0)
        store_half(hp, mu, at, ahead)
        store_half(bl, mu, at, mat_vec(load_link(mu, at), ahead, True))

    arrived(0)
    arrived(4)
    for_each(chunks, lambda v: project(3, v))

    for c in range(12):
        face_out[0, c, 0:face_t, :] = hm[3, c, 0:face_t, :]
        face_out[1, c, 0:face_t, :] = bl[3, c, rows - face_t:rows, :]
    pl.semaphore_wait(barrier, 4)
    sends[0].start()
    sends[1].start()
    arrived(3)
    for_each(chunks, lambda v: project(2, v))
    for c in range(12):
        face_out[2, c, 0:face_z, :] = hm[2, c, pl.ds(0, face_z, nz), :]
        face_out[3, c, 0:face_z, :] = bl[2, c, pl.ds(nz - 1, face_z, nz), :]
    sends[2].start()
    sends[3].start()

    arrived(1)
    for_each(chunks, lambda v: project(0, v))
    arrived(2)
    for_each(chunks, lambda v: project(1, v))

    def shifts(c):
        sh_hm[0, c] = shift_x1(hm[0, c], 1)
        sh_bl[0, c] = shift_x1(bl[0, c], -1)
        sh_hm[1, c] = shift_x2(hm[1, c], 1)
        sh_bl[1, c] = shift_x2(bl[1, c], -1)
        z_ahead(hm, sh_hm, c)
        z_behind(bl, sh_bl, c)
        t_ahead(hm, sh_hm, c)
        t_behind(bl, sh_bl, c)

    for_each(12, shifts)

    def hop(mu, at, total):
        ahead = mat_vec(load_link(mu, at), load_half(sh_hm, mu, at), False)
        store_half(prod, mu, at, ahead)
        total = add_whole(mu, total, ahead, -1.0)
        return add_whole(mu, total, load_half(sh_bl, mu, at), 1.0)

    zero = jnp.zeros((TILE, LANES), jnp.float32)

    arrived(5)

    def local(v):
        at = window(v)
        field = load_spinor(psi, at)
        total = [[(zero, zero)] * 3 for _ in range(4)]
        for mu in (0, 1):
            total = hop(mu, at, total)
        for s in range(4):
            for c in range(3):
                base = 36 * (s // 2) + 6 * (3 * (s % 2) + c)
                re = (4.0 + bare_mass) * field[s][c][0] - 0.5 * total[s][c][0]
                im = (4.0 + bare_mass) * field[s][c][1] - 0.5 * total[s][c][1]
                for k in range(6):
                    other = field[2 * (s // 2) + k // 3][k % 3]
                    c_re = clov[base + k, at, :]
                    c_im = clov[72 + base + k, at, :]
                    re = re + (c_re * other[0] - c_im * other[1])
                    im = im + (c_re * other[1] + c_im * other[0])
                acc[3 * s + c, at, :] = re
                acc[12 + 3 * s + c, at, :] = im

    for_each(chunks, local)

    for k in range(4):
        sends[k].wait_recv()

    for c in range(12):
        sh_hm[3, c, pl.ds(rows - face_t, face_t), :] = face_in[0, c, 0:face_t, :] * high_sign
        sh_bl[3, c, pl.ds(0, face_t), :] = face_in[1, c, 0:face_t, :] * low_sign
        sh_hm[2, c, pl.ds(nz - 1, face_z, nz), :] = face_in[2, c, 0:face_z, :]
        sh_bl[2, c, pl.ds(0, face_z, nz), :] = face_in[3, c, 0:face_z, :]

    def finish(v):
        at = window(v)
        total = [[(zero, zero)] * 3 for _ in range(4)]
        for mu in (2, 3):
            total = hop(mu, at, total)
        held = load_spinor(acc, at)
        phi = [
            [(held[s][c][0] - 0.5 * total[s][c][0], held[s][c][1] - 0.5 * total[s][c][1]) for c in range(3)]
            for s in range(4)
        ]
        for s in range(4):
            for c in range(3):
                out_ref[3 * s + c, at, :] = phi[s][c][0]
                out_ref[12 + 3 * s + c, at, :] = phi[s][c][1]
        for mu in range(4):
            store_half(hphi, mu, at, half(mu, phi, 1.0))

    for_each(chunks, finish)

    for c in range(12):
        face_out[4, c, 0:face_t, :] = hphi[3, c, 0:face_t, :]
        face_out[5, c, 0:face_z, :] = hphi[2, c, pl.ds(0, face_z, nz), :]
    sends[4].start()
    sends[5].start()

    leave(0)

    def shifts_phi(c):
        sh_hphi[0, c] = shift_x1(hphi[0, c], 1)
        sh_hphi[1, c] = shift_x2(hphi[1, c], 1)
        z_ahead(hphi, sh_hphi, c)
        t_ahead(hphi, sh_hphi, c)

    for_each(12, shifts_phi)

    def force(mu, v):
        at = window(v)
        second = mat_vec(load_link(mu, at), load_half(sh_hphi, mu, at), False)
        second_right = load_half(hp, mu, at)
        first = load_half(prod, mu, at)
        first_right = half(mu, load_spinor(out_ref, at), -1.0)
        pairs = [(first[s], first_right[s]) for s in range(2)] + [(second[s], second_right[s]) for s in range(2)]

        def w_re(a, b):
            return csum([l[a][0] * r[b][0] + l[a][1] * r[b][1] for l, r in pairs])

        def w_im(a, b):
            return csum([l[a][1] * r[b][0] - l[a][0] * r[b][1] for l, r in pairs])

        diag = [w_im(a, a) for a in range(3)]
        third = (diag[0] + diag[1] + diag[2]) * (1.0 / 3.0)
        base = 18 * mu
        for a in range(3):
            force_ref[base + 4 * a, at, :] = zero
            force_ref[base + 9 + 4 * a, at, :] = diag[a] - third
            for b in range(a + 1, 3):
                re = 0.5 * (w_re(a, b) - w_re(b, a))
                im = 0.5 * (w_im(a, b) + w_im(b, a))
                force_ref[base + 3 * a + b, at, :] = re
                force_ref[base + 3 * b + a, at, :] = -re
                force_ref[base + 9 + 3 * a + b, at, :] = im
                force_ref[base + 9 + 3 * b + a, at, :] = im

    for mu in (0, 1):
        for_each(chunks, lambda v: force(mu, v))
        leave(1 + mu)

    for k in (4, 5):
        sends[k].wait_recv()
    for c in range(12):
        sh_hphi[3, c, pl.ds(rows - face_t, face_t), :] = face_in[4, c, 0:face_t, :] * high_sign
        sh_hphi[2, c, pl.ds(nz - 1, face_z, nz), :] = face_in[5, c, 0:face_z, :]
    for mu in (2, 3):
        for_each(chunks, lambda v: force(mu, v))
        leave(1 + mu)
    for k in range(6):
        sends[k].wait_send()
    for n in range(5):
        left(n)


def body(spinor, links, clover):
    nt, nz = spinor.shape[3], spinor.shape[4]
    sites = spinor.shape[-3:]
    x, u, c = (a.reshape((-1,) + sites) for a in (spinor, links, clover))
    parts = nt * (sites[2] // LANES)
    rows = parts * nz
    face = max(rows // nt, rows // nz)

    def halves():
        return pltpu.VMEM((4, 12, rows, LANES), jnp.float32)

    def held(array):
        return pltpu.VMEM((array.shape[0], parts, nz, LANES), jnp.float32)

    applied, force = pl.pallas_call(
        lambda *refs: kernel(nt, nz, *refs),
        name="wilson",
        out_shape=(
            jax.ShapeDtypeStruct(x.shape, jnp.float32),
            jax.ShapeDtypeStruct(u.shape, jnp.float32),
        ),
        in_specs=[pl.BlockSpec(memory_space=pl.ANY)] * 3,
        out_specs=(pl.BlockSpec(memory_space=pl.ANY),) * 2,
        scratch_shapes=[
            held(x), held(u), held(c), held(x), held(u),
            halves(), halves(), halves(), halves(), halves(), halves(),
            pltpu.VMEM((24, rows, LANES), jnp.float32),
            halves(), halves(),
            pltpu.VMEM((6, 12, face, LANES), jnp.float32),
            pltpu.VMEM((6, 12, face, LANES), jnp.float32),
            pltpu.SemaphoreType.DMA((6,)),
            pltpu.SemaphoreType.DMA((5,)),
            pltpu.SemaphoreType.DMA((6,)),
            pltpu.SemaphoreType.DMA((6,)),
        ],
        compiler_params=pltpu.CompilerParams(collective_id=0, has_side_effects=True),
    )(x, u, c)
    return applied.reshape(spinor.shape), force.reshape(links.shape)


def solution(mesh):
    return jax.shard_map(
        body,
        mesh=mesh,
        in_specs=(
            P(None, None, None, "ta", "gz", None),
            P(None, None, None, None, "ta", "gz", None),
            P(None, None, None, None, "ta", "gz", None),
        ),
        out_specs=(
            P(None, None, None, "ta", "gz", None),
            P(None, None, None, None, "ta", "gz", None),
        ),
        check_vma=False,
    )
```

```python
import jax
import jax.numpy as jnp
from jax import lax
from jax.experimental import pallas as pl
from jax.experimental.pallas import tpu as pltpu
from jax.sharding import PartitionSpec as P

NX = 64
LANES = 128
TILE = 8
MESH = pl.DeviceIdType.MESH

bare_mass = -0.25
gamma_table = (
    ((3, 0.0, -1.0), (2, 0.0, -1.0), (1, 0.0, 1.0), (0, 0.0, 1.0)),
    ((3, -1.0, 0.0), (2, 1.0, 0.0), (1, 1.0, 0.0), (0, -1.0, 0.0)),
    ((2, 0.0, -1.0), (3, 0.0, 1.0), (0, 0.0, 1.0), (1, 0.0, -1.0)),
    ((2, 1.0, 0.0), (3, 1.0, 0.0), (0, 1.0, 0.0), (1, 1.0, 0.0)),
)


def add_signed(a, b, positive):
    return a + b if positive else a - b


def add_phase(a, b, phase_re, phase_im):
    if phase_im == 0.0:
        up = phase_re > 0
        return (add_signed(a[0], b[0], up), add_signed(a[1], b[1], up))
    up = phase_im > 0
    return (add_signed(a[0], b[1], not up), add_signed(a[1], b[0], up))


def half(mu, field, sign):
    out = []
    for s in range(2):
        source, p_re, p_im = gamma_table[mu][s]
        out.append(
            [add_phase(field[s][c], field[source][c], sign * p_re, sign * p_im) for c in range(3)]
        )
    return out


def add_whole(mu, total, halves, sign):
    out = [[add_phase(total[s][c], halves[s][c], 1.0, 0.0) for c in range(3)] for s in range(2)]
    for s in (2, 3):
        source, p_re, p_im = gamma_table[mu][s]
        out.append(
            [add_phase(total[s][c], halves[source][c], sign * p_re, sign * p_im) for c in range(3)]
        )
    return out


def csum(terms):
    total = terms[0]
    for term in terms[1:]:
        total = total + term
    return total


def mat_vec(link, vec, dagger):
    out = []
    for s in range(2):
        rows = []
        for a in range(3):
            re, im = [], []
            for b in range(3):
                h = vec[s][b]
                if dagger:
                    m = link[b][a]
                    re.append(m[0] * h[0] + m[1] * h[1])
                    im.append(m[0] * h[1] - m[1] * h[0])
                else:
                    m = link[a][b]
                    re.append(m[0] * h[0] - m[1] * h[1])
                    im.append(m[0] * h[1] + m[1] * h[0])
            rows.append((csum(re), csum(im)))
        out.append(rows)
    return out


def flat(ref):
    return ref.reshape(ref.shape[0], ref.shape[1] * ref.shape[2], ref.shape[3])


def parts_of(whole, held):
    parts = whole.shape[-1] // LANES
    for t in range(whole.shape[-3]):
        for q in range(parts):
            yield whole.at[:, t, :, pl.ds(LANES * q, LANES)], held.at[:, parts * t + q]


def kernel(nt, nz, x_hbm, u_hbm, c_hbm, out_hbm, force_hbm, psi_in, link_in, clov_in, phi_out, force_out, hm, hp, bl,
           sh_hm, sh_bl, prod, acc, hphi, sh_hphi, face_out, face_in, in_sem, out_sem, send_sem, recv_sem):
    psi, link, clov, out_ref, force_ref = map(flat, (psi_in, link_in, clov_in, phi_out, force_out))
    rows = psi.shape[1]
    face_t = rows // nt
    face_z = rows // nz
    chunks = rows // TILE
    t_place, z_place = lax.axis_index("ta"), lax.axis_index("gz")
    t_count, z_count = lax.axis_size("ta"), lax.axis_size("gz")
    t_next = (lax.rem(t_place + 1, t_count), z_place)
    t_prev = (lax.rem(t_place + t_count - 1, t_count), z_place)
    z_next = (t_place, lax.rem(z_place + 1, z_count))
    z_prev = (t_place, lax.rem(z_place + z_count - 1, z_count))
    low_sign = jnp.where(t_place == 0, -1.0, 1.0).astype(jnp.float32)
    high_sign = jnp.where(t_place == t_count - 1, -1.0, 1.0).astype(jnp.float32)

    barrier = pltpu.get_barrier_semaphore()
    for target in (t_next, t_prev, z_next, z_prev):
        pl.semaphore_signal(barrier, inc=1, device_id=target, device_id_type=MESH)

    groups = [(x_hbm, psi_in)]
    for mu in range(4):
        part = pl.ds(18 * mu, 18)
        groups.append((u_hbm.at[part], link_in.at[part]))
    groups.append((c_hbm, clov_in))
    for n in (0, 3, 4, 1, 2, 5):
        for src, dst in parts_of(*groups[n]):
            pltpu.make_async_copy(src, dst, in_sem.at[n]).start()

    def arrived(n):
        held = groups[n][1]
        pltpu.make_async_copy(held, held, in_sem.at[n]).wait()

    results = [(out_hbm, phi_out)]
    for mu in range(4):
        part = pl.ds(18 * mu, 18)
        results.append((force_hbm.at[part], force_out.at[part]))

    def leave(n):
        for dst, src in parts_of(*results[n]):
            pltpu.make_async_copy(src, dst, out_sem.at[n]).start()

    def left(n):
        held = results[n][1]
        pltpu.make_async_copy(held, held, out_sem.at[n]).wait()

    def window(v):
        return pl.ds(pl.multiple_of(v * TILE, TILE), TILE)

    def load_spinor(ref, at):
        return [[(ref[3 * s + c, at, :], ref[12 + 3 * s + c, at, :]) for c in range(3)] for s in range(4)]

    def load_half(ref, mu, at):
        return [[(ref[mu, 3 * s + c, at, :], ref[mu, 6 + 3 * s + c, at, :]) for c in range(3)] for s in range(2)]

    def store_half(ref, mu, at, value):
        for s in range(2):
            for c in range(3):
                ref[mu, 3 * s + c, at, :] = value[s][c][0]
                ref[mu, 6 + 3 * s + c, at, :] = value[s][c][1]

    def load_link(mu, at):
        return [[(link[18 * mu + 3 * a + b, at, :], link[18 * mu + 9 + 3 * a + b, at, :]) for b in range(3)] for a in range(3)]

    lane = lax.broadcasted_iota(jnp.int32, (rows, LANES), 1)
    row = lax.broadcasted_iota(jnp.int32, (rows, LANES), 0)
    lane_in = lax.rem(lane, NX)
    row_in = lax.rem(row, face_t)
    upper = lane >= NX

    def shift_x1(value, step):
        if step == 1:
            near, far = pltpu.roll(value, LANES - 1, 1), pltpu.roll(value, NX - 1, 1)
            return jnp.where(lane_in == NX - 1, far, near)
        near, far = pltpu.roll(value, 1, 1), pltpu.roll(value, LANES - NX + 1, 1)
        return jnp.where(lane_in == 0, far, near)

    def shift_x2(value, step):
        turned = pltpu.roll(value, NX, 1)
        if step == 1:
            near = pltpu.roll(turned, rows - nz, 0)
            far = pltpu.roll(turned, face_t - nz, 0)
            moved = jnp.where(row_in >= face_t - nz, far, near)
            return jnp.where(upper, moved, turned)
        near = pltpu.roll(turned, nz, 0)
        far = pltpu.roll(turned, rows - face_t + nz, 0)
        moved = jnp.where(row_in < nz, far, near)
        return jnp.where(upper, turned, moved)

    def z_ahead(src, dst, c):
        for z in range(nz - 1):
            dst[2, c, pl.ds(z, face_z, nz), :] = src[2, c, pl.ds(z + 1, face_z, nz), :]

    def z_behind(src, dst, c):
        for z in range(1, nz):
            dst[2, c, pl.ds(z, face_z, nz), :] = src[2, c, pl.ds(z - 1, face_z, nz), :]

    def t_ahead(src, dst, c):
        dst[3, c, pl.ds(0, rows - face_t), :] = src[3, c, pl.ds(face_t, rows - face_t), :]

    def t_behind(src, dst, c):
        dst[3, c, pl.ds(face_t, rows - face_t), :] = src[3, c, pl.ds(0, rows - face_t), :]

    def for_each(count, body):
        def step(i, carry):
            body(i)
            return carry

        lax.fori_loop(0, count, step, 0)

    targets = (t_prev, t_next, z_prev, z_next, t_prev, z_prev)
    sends = [
        pltpu.make_async_remote_copy(
            src_ref=face_out.at[k], dst_ref=face_in.at[k], send_sem=send_sem.at[k],
            recv_sem=recv_sem.at[k], device_id=targets[k], device_id_type=MESH,
        )
        for k in range(6)
    ]

    def project(mu, v):
        at = window(v)
        field = load_spinor(psi, at)
        store_half(hm, mu, at, half(mu, field, -1.0))
        ahead = half(mu, field, 1.0)
        store_half(hp, mu, at, ahead)
        store_half(bl, mu, at, mat_vec(load_link(mu, at), ahead, True))

    def face(k, c, size):
        return k, pl.ds(c * size, size)

    arrived(0)
    arrived(3)
    for_each(chunks, lambda v: project(2, v))
    for c in range(12):
        k, at = face(3, c, face_z)
        face_out[k, at, :] = bl[2, c, pl.ds(nz - 1, face_z, nz), :]
    pl.semaphore_wait(barrier, 4)
    sends[3].start()
    for c in range(12):
        k, at = face(2, c, face_z)
        face_out[k, at, :] = hm[2, c, pl.ds(0, face_z, nz), :]
    arrived(4)
    for_each(chunks, lambda v: project(3, v))
    for c in range(12):
        k, at = face(0, c, face_t)
        face_out[k, at, :] = hm[3, c, 0:face_t, :]
        k, at = face(1, c, face_t)
        face_out[k, at, :] = bl[3, c, rows - face_t:rows, :]
    sends[1].start()
    sends[0].start()
    sends[2].start()

    arrived(1)
    for_each(chunks, lambda v: project(0, v))
    arrived(2)
    for_each(chunks, lambda v: project(1, v))

    def shifts(c):
        sh_hm[0, c] = shift_x1(hm[0, c], 1)
        sh_bl[0, c] = shift_x1(bl[0, c], -1)
        sh_hm[1, c] = shift_x2(hm[1, c], 1)
        sh_bl[1, c] = shift_x2(bl[1, c], -1)
        z_ahead(hm, sh_hm, c)
        z_behind(bl, sh_bl, c)
        t_ahead(hm, sh_hm, c)
        t_behind(bl, sh_bl, c)

    for_each(12, shifts)

    def hop(mu, at, total):
        ahead = mat_vec(load_link(mu, at), load_half(sh_hm, mu, at), False)
        store_half(prod, mu, at, ahead)
        total = add_whole(mu, total, ahead, -1.0)
        return add_whole(mu, total, load_half(sh_bl, mu, at), 1.0)

    zero = jnp.zeros((TILE, LANES), jnp.float32)

    arrived(5)

    def local(v):
        at = window(v)
        field = load_spinor(psi, at)
        total = [[(zero, zero)] * 3 for _ in range(4)]
        for mu in (0, 1):
            total = hop(mu, at, total)
        for s in range(4):
            for c in range(3):
                base = 36 * (s // 2) + 6 * (3 * (s % 2) + c)
                re = (4.0 + bare_mass) * field[s][c][0] - 0.5 * total[s][c][0]
                im = (4.0 + bare_mass) * field[s][c][1] - 0.5 * total[s][c][1]
                for k in range(6):
                    other = field[2 * (s // 2) + k // 3][k % 3]
                    c_re = clov[base + k, at, :]
                    c_im = clov[72 + base + k, at, :]
                    re = re + (c_re * other[0] - c_im * other[1])
                    im = im + (c_re * other[1] + c_im * other[0])
                acc[3 * s + c, at, :] = re
                acc[12 + 3 * s + c, at, :] = im

    for_each(chunks, local)

    for k in (0, 1, 3):
        sends[k].wait_recv()
    for c in range(12):
        k, at = face(0, c, face_t)
        sh_hm[3, c, pl.ds(rows - face_t, face_t), :] = face_in[k, at, :] * high_sign
        k, at = face(1, c, face_t)
        sh_bl[3, c, pl.ds(0, face_t), :] = face_in[k, at, :] * low_sign
        k, at = face(3, c, face_z)
        sh_bl[2, c, pl.ds(0, face_z, nz), :] = face_in[k, at, :]
        sh_hm[2, c, pl.ds(nz - 1, face_z, nz), :] = jnp.zeros((face_z, LANES), jnp.float32)

    def finish(v, early):
        at = window(v)
        total = [[(zero, zero)] * 3 for _ in range(4)]
        for mu in (2, 3):
            total = hop(mu, at, total)
        held = load_spinor(acc, at)
        phi = [
            [(held[s][c][0] - 0.5 * total[s][c][0], held[s][c][1] - 0.5 * total[s][c][1]) for c in range(3)]
            for s in range(4)
        ]
        if early:
            store_half(hphi, 2, at, half(2, phi, 1.0))
            return
        for s in range(4):
            for c in range(3):
                out_ref[3 * s + c, at, :] = phi[s][c][0]
                out_ref[12 + 3 * s + c, at, :] = phi[s][c][1]
        for mu in range(4):
            store_half(hphi, mu, at, half(mu, phi, 1.0))

    for_each(chunks, lambda v: finish(v, True))
    for c in range(12):
        k, at = face(5, c, face_z)
        face_out[k, at, :] = hphi[2, c, pl.ds(0, face_z, nz), :]
    sends[5].start()

    sends[2].wait_recv()
    for c in range(12):
        k, at = face(2, c, face_z)
        sh_hm[2, c, pl.ds(nz - 1, face_z, nz), :] = face_in[k, at, :]
    for_each(chunks, lambda v: finish(v, False))
    for c in range(12):
        k, at = face(4, c, face_t)
        face_out[k, at, :] = hphi[3, c, 0:face_t, :]
    sends[4].start()
    leave(0)

    def shifts_phi(c):
        sh_hphi[0, c] = shift_x1(hphi[0, c], 1)
        sh_hphi[1, c] = shift_x2(hphi[1, c], 1)
        z_ahead(hphi, sh_hphi, c)
        t_ahead(hphi, sh_hphi, c)

    for_each(12, shifts_phi)

    def force(mu, v):
        at = window(v)
        second = mat_vec(load_link(mu, at), load_half(sh_hphi, mu, at), False)
        second_right = load_half(hp, mu, at)
        first = load_half(prod, mu, at)
        first_right = half(mu, load_spinor(out_ref, at), -1.0)
        pairs = [(first[s], first_right[s]) for s in range(2)] + [(second[s], second_right[s]) for s in range(2)]

        def w_re(a, b):
            return csum([l[a][0] * r[b][0] + l[a][1] * r[b][1] for l, r in pairs])

        def w_im(a, b):
            return csum([l[a][1] * r[b][0] - l[a][0] * r[b][1] for l, r in pairs])

        diag = [w_im(a, a) for a in range(3)]
        third = (diag[0] + diag[1] + diag[2]) * (1.0 / 3.0)
        base = 18 * mu
        for a in range(3):
            force_ref[base + 4 * a, at, :] = zero
            force_ref[base + 9 + 4 * a, at, :] = diag[a] - third
            for b in range(a + 1, 3):
                re = 0.5 * (w_re(a, b) - w_re(b, a))
                im = 0.5 * (w_im(a, b) + w_im(b, a))
                force_ref[base + 3 * a + b, at, :] = re
                force_ref[base + 3 * b + a, at, :] = -re
                force_ref[base + 9 + 3 * a + b, at, :] = im
                force_ref[base + 9 + 3 * b + a, at, :] = im

    for mu in (0, 1):
        for_each(chunks, lambda v: force(mu, v))
        leave(1 + mu)

    sends[4].wait_recv()
    for c in range(12):
        k, at = face(4, c, face_t)
        sh_hphi[3, c, pl.ds(rows - face_t, face_t), :] = face_in[k, at, :] * high_sign
    for_each(chunks, lambda v: force(3, v))
    leave(4)
    sends[5].wait_recv()
    for c in range(12):
        k, at = face(5, c, face_z)
        sh_hphi[2, c, pl.ds(nz - 1, face_z, nz), :] = face_in[k, at, :]
    for_each(chunks, lambda v: force(2, v))
    leave(3)
    for k in range(6):
        sends[k].wait_send()
    for n in range(5):
        left(n)


def body(spinor, links, clover):
    nt, nz = spinor.shape[3], spinor.shape[4]
    sites = spinor.shape[-3:]
    x, u, c = (a.reshape((-1,) + sites) for a in (spinor, links, clover))
    parts = nt * (sites[2] // LANES)
    rows = parts * nz
    face = max(rows // nt, rows // nz)

    def halves():
        return pltpu.VMEM((4, 12, rows, LANES), jnp.float32)

    def held(array):
        return pltpu.VMEM((array.shape[0], parts, nz, LANES), jnp.float32)

    applied, force = pl.pallas_call(
        lambda *refs: kernel(nt, nz, *refs),
        name="wilson",
        out_shape=(
            jax.ShapeDtypeStruct(x.shape, jnp.float32),
            jax.ShapeDtypeStruct(u.shape, jnp.float32),
        ),
        in_specs=[pl.BlockSpec(memory_space=pl.ANY)] * 3,
        out_specs=(pl.BlockSpec(memory_space=pl.ANY),) * 2,
        scratch_shapes=[
            held(x), held(u), held(c), held(x), held(u),
            halves(), halves(), halves(), halves(), halves(), halves(),
            pltpu.VMEM((24, rows, LANES), jnp.float32),
            halves(), halves(),
            pltpu.VMEM((6, 12 * face, LANES), jnp.float32),
            pltpu.VMEM((6, 12 * face, LANES), jnp.float32),
            pltpu.SemaphoreType.DMA((6,)),
            pltpu.SemaphoreType.DMA((5,)),
            pltpu.SemaphoreType.DMA((6,)),
            pltpu.SemaphoreType.DMA((6,)),
        ],
        compiler_params=pltpu.CompilerParams(collective_id=0, has_side_effects=True),
    )(x, u, c)
    return applied.reshape(spinor.shape), force.reshape(links.shape)


def solution(mesh):
    return jax.shard_map(
        body,
        mesh=mesh,
        in_specs=(
            P(None, None, None, "ta", "gz", None),
            P(None, None, None, None, "ta", "gz", None),
            P(None, None, None, None, "ta", "gz", None),
        ),
        out_specs=(
            P(None, None, None, "ta", "gz", None),
            P(None, None, None, None, "ta", "gz", None),
        ),
        check_vma=False,
    )
```
